32 devices in a mesh: delay: 4 (over z), row: 4 (over x, core), col: 2 (over y).
Axes of the slice: x: 2, y: 2, z: 4, core: 2. Of those that a mesh axis runs over, the one named last changes fastest.
Arguments:
- operators: float32 [4, 9216, 9216], P('delay', 'col', 'row'), may hold values from -0.0625 to 0.0625
- excitation: float32 [3, 9216, 256], P(None, 'col'), may hold values from -6 to 6
- pending: float32 [4, 9216, 256], P('delay', 'col', 'row'), may hold values from -6 to 6
- sheet_gain: float32 [9216], P('row'), may hold values from 0.2 to 2
Outputs:
- currents: float32 [3, 9216, 256], P(None, 'row', 'col')
- remaining: float32 [4, 9216, 256], P('delay', 'col', 'row')
The draws below stay inside these ranges and needn't reach their ends.
All inputs are finite; a program needn't handle non-finite values.
Results may differ from the reference program's by a relative error of at most 0.00014.
Values sent between devices are 32-bit elements; how exact they have to be, the bound alone decides.
A program may use at most 128 MiB of HBM per device.

```python
import math
import jax
import jax.numpy as jnp
from jax import lax

ORDER = 9216
COLUMNS = 256
STEPS = 3
DELAYS = 4


def steps_of(rng, shape, split, low, high):
    loudness = 1.0
    for position, shards_of in split:
        steps = jax.random.uniform(jax.random.fold_in(jax.random.fold_in(rng, 6), position), (shards_of,), jnp.float32, low / len(split), high / len(split))
        loudness = loudness * jnp.repeat(jnp.exp(steps), shape[position] // shards_of).reshape((-1,) + (1,) * (len(shape) - 1 - position))
    return loudness


def normal_values(key, shape, deviation, bound, split=(), kind=jnp.bfloat16):
    drawn = jax.random.normal(key, shape, jnp.float32) * deviation
    if len(split) > 0:
        drawn = steps_of(key, shape, split, -0.22, 0.18) * drawn
    return jnp.clip(drawn, min=-bound, max=bound).astype(kind)


def setup_inputs(seed: int = 0) -> dict:
    keys = jax.random.split(jax.random.key(seed), 5)
    return {
        "operators": normal_values(keys[0], (DELAYS, ORDER, ORDER), ORDER ** -0.5, 0.0625, ((0, 4), (1, 2), (2, 4)), jnp.float32),
        "excitation": normal_values(keys[1], (STEPS, ORDER, COLUMNS), 1.0, 6.0, ((1, 2),), jnp.float32),
        "pending": normal_values(keys[2], (DELAYS, ORDER, COLUMNS), 1.0, 6.0, ((0, 4), (1, 2), (2, 4)), jnp.float32),
        "sheet_gain": jnp.clip(jnp.exp(math.log(2.0) - 2.3025851 * jax.random.uniform(keys[3], (ORDER,), jnp.float32) ** steps_of(keys[3], (ORDER,), ((0, 4),), -0.2, 0.2)), 0.2, 2.0),
    }


def reference(operators, excitation, pending, sheet_gain):
    future = pending
    outputs = []
    for moment in range(STEPS):
        driving = excitation[moment] - future[0]
        sheet = jnp.dot(operators[0].T, driving, precision=lax.Precision.HIGHEST)
        current = sheet / (1.0 + sheet_gain[:, None] * sheet * sheet)
        outputs.append(current)
        updated = [future[0]]
        for delay_slot in range(1, DELAYS):
            updated.append(future[delay_slot] + jnp.dot(operators[delay_slot], current, precision=lax.Precision.HIGHEST))
        updated.append(jnp.zeros_like(future[0]))
        future = jnp.stack(updated[1:])
    return jnp.stack(outputs), future
```

```python
import jax
import jax.numpy as jnp
from jax import lax
from jax.sharding import PartitionSpec as P

STEPS = 3
CHUNKS = 2
SKEW = 1
AXES = ("delay", "row", "col")


def local(operators, excitation, pending, sheet_gain):
    block = operators[0]
    groups, rows, cols = (lax.axis_size(a) for a in AXES)
    d, r, c = (lax.axis_index(a) for a in AXES)
    is_head = d == 0
    tests, basis = block.shape
    finest = max(rows, cols)
    width = excitation.shape[2] // (finest * CHUNKS)
    stages = STEPS * CHUNKS
    slots = stages + SKEW * (groups - 1)

    def place(dd, rr, cc):
        return (dd * rows + rr) * cols + cc

    def active(s):
        return [dd for dd in range(groups) if 0 <= s - SKEW * dd < stages]

    def exchange(x, axis, bit, members):
        pairs = []
        for dd in members:
            for rr in range(rows):
                for cc in range(cols):
                    to = (dd, rr ^ bit, cc) if axis == "row" else (dd, rr, cc ^ bit)
                    pairs.append((place(dd, rr, cc), place(*to)))
        return lax.ppermute(x, AXES, pairs)

    def shift(x, step, members):
        pairs = [
            (place(dd, rr, cc), place(dd + step, rr, cc))
            for dd in members
            if 0 <= dd + step < groups
            for rr in range(rows)
            for cc in range(cols)
        ]
        return lax.ppermute(x, AXES, pairs) if pairs else jnp.zeros_like(x)

    def scatter_sum(x, axis, members):
        n = lax.axis_size(axis)
        at = r if axis == "row" else c
        w = x.shape[0] // n
        x = x.reshape(n, w, -1)
        bit = 1
        while bit < n:
            x = x.reshape(x.shape[0] // 2, 2, w, -1)
            mine = (at // bit) % 2
            kept = lax.dynamic_index_in_dim(x, mine, 1, keepdims=False)
            other = lax.dynamic_index_in_dim(x, 1 - mine, 1, keepdims=False)
            x = kept + exchange(other, axis, bit, members)
            bit *= 2
        return x[0]

    def gather(x, axis, members):
        n = lax.axis_size(axis)
        at = r if axis == "row" else c
        w, length = x.shape
        x = x[None]
        bit = n // 2
        while bit:
            got = exchange(x, axis, bit, members)
            mine = (at // bit) % 2
            low = jnp.where(mine == 0, x, got)
            high = jnp.where(mine == 0, got, x)
            x = jnp.stack([low, high], axis=1).reshape(-1, w, length)
            bit //= 2
        return x.reshape(n * w, length)

    def product(a, dims):
        return lax.dot_general(
            a, block, (dims, ((), ())), precision=lax.Precision.HIGH, preferred_element_type=jnp.float32
        )

    driven = excitation.transpose(0, 2, 1).reshape(STEPS, finest, CHUNKS, width, tests)
    driven = lax.optimization_barrier(driven.transpose(0, 2, 1, 3, 4))
    waiting = pending[0].T.reshape(finest // rows, CHUNKS, width, tests)
    gain = sheet_gain[None, :]
    held, updated, arrived = [], [], {}

    def future_at(s):
        stage = s - SKEW * d
        source = s - CHUNKS + SKEW
        got = shift(updated[source], -1, [dd for dd in active(source) if dd > 0]) if source >= 0 else None
        arrived[s] = got
        if s >= CHUNKS + SKEW * (groups - 1):
            return got
        first = lax.dynamic_index_in_dim(waiting, jnp.clip(stage, 0, CHUNKS - 1), 1, keepdims=False)
        first = first.reshape(-1, tests)
        return first if got is None else jnp.where(stage < CHUNKS, first, got)

    for s in range(slots):
        members = active(s)
        tail = [dd for dd in members if dd > 0]
        future = future_at(s)
        current = shift(held[s - SKEW], 1, active(s - SKEW)) if s >= SKEW else None
        driving = whole = None
        if 0 in members:
            driving = gather(future, "row", [0])
        if tail:
            whole = gather(current, "col", tail)
        driving, whole, future, current = lax.optimization_barrier((driving, whole, future, current))
        fresh, new = current, future
        if driving is not None:
            driving = driven[s // CHUNKS, s % CHUNKS].reshape(-1, tests) - driving
            part = lax.cond(
                is_head,
                lambda x: product(x, ((1,), (0,))),
                lambda x: jnp.zeros((x.shape[0], basis), jnp.float32),
                driving,
            )
        if whole is not None:
            field = lax.cond(
                is_head,
                lambda x: jnp.zeros((x.shape[0], tests), jnp.float32),
                lambda x: product(x, ((1,), (1,))),
                whole,
            )
        if driving is not None:
            sheet = scatter_sum(part, "col", [0])
            fresh = sheet / (1.0 + gain * sheet * sheet)
            if current is not None:
                fresh = jnp.where(is_head, fresh, current)
        if whole is not None:
            new = future + scatter_sum(field, "row", tail)
        fresh, new = lax.optimization_barrier((fresh, new))
        held.append(fresh)
        updated.append(new)

    for s in range(slots, stages + CHUNKS + SKEW * (groups - 2)):
        future_at(s)

    def outputs_of(dd):
        def build(held, got):
            mine = held[SKEW * dd : SKEW * dd + stages]
            now = jnp.stack(mine).reshape(STEPS, CHUNKS, finest // cols, width, basis)
            now = now.transpose(0, 4, 2, 1, 3).reshape(STEPS, basis, -1)
            if dd == groups - 1:
                return now, jnp.zeros((1, tests, pending.shape[2]), jnp.float32)
            last = [got[stages + SKEW * dd + i - stages] for i in range(CHUNKS)]
            last = jnp.stack(last).reshape(CHUNKS, finest // rows, width, tests)
            return now, last.transpose(3, 1, 0, 2).reshape(1, tests, -1)

        return build

    got = [arrived[s] for s in range(stages, stages + CHUNKS + SKEW * (groups - 2))]
    return lax.switch(d, [outputs_of(dd) for dd in range(groups)], held, got)


def solution(mesh):
    in_specs = (P("delay", "col", "row"), P(None, "col", None), P("delay", "col", "row"), P("row"))
    out_specs = (P(None, "row", "col"), P("delay", "col", "row"))
    return jax.shard_map(local, mesh=mesh, in_specs=in_specs, out_specs=out_specs, check_vma=False)
```

```python
import jax
import jax.numpy as jnp
from jax import lax
from jax.sharding import PartitionSpec as P

STEPS = 3
CHUNKS = 2
SKEW = 1
AXES = ("delay", "row", "col")


def local(operators, excitation, pending, sheet_gain):
    block = operators[0]
    groups, rows, cols = (lax.axis_size(a) for a in AXES)
    d, r, c = (lax.axis_index(a) for a in AXES)
    is_head = d == 0
    tests, basis = block.shape
    finest = max(rows, cols)
    width = excitation.shape[2] // (finest * CHUNKS)
    stages = STEPS * CHUNKS
    slots = stages + SKEW * (groups - 1)

    def place(dd, rr, cc):
        return (dd * rows + rr) * cols + cc

    def active(s):
        return [dd for dd in range(groups) if 0 <= s - SKEW * dd < stages]

    def exchange(x, axis, bit, members):
        pairs = []
        for dd in members:
            for rr in range(rows):
                for cc in range(cols):
                    to = (dd, rr ^ bit, cc) if axis == "row" else (dd, rr, cc ^ bit)
                    pairs.append((place(dd, rr, cc), place(*to)))
        return lax.ppermute(x, AXES, pairs)

    def shift(x, step, members):
        pairs = [
            (place(dd, rr, cc), place(dd + step, rr, cc))
            for dd in members
            if 0 <= dd + step < groups
            for rr in range(rows)
            for cc in range(cols)
        ]
        return lax.ppermute(x, AXES, pairs) if pairs else jnp.zeros_like(x)

    def scatter_sum(x, axis, members):
        n = lax.axis_size(axis)
        at = r if axis == "row" else c
        w = x.shape[0] // n
        x = x.reshape(n, w, -1)
        bit = 1
        while bit < n:
            x = x.reshape(x.shape[0] // 2, 2, w, -1)
            mine = (at // bit) % 2
            kept = lax.dynamic_index_in_dim(x, mine, 1, keepdims=False)
            other = lax.dynamic_index_in_dim(x, 1 - mine, 1, keepdims=False)
            x = kept + exchange(other, axis, bit, members)
            bit *= 2
        return x[0]

    def gather(x, axis, members):
        n = lax.axis_size(axis)
        at = r if axis == "row" else c
        w, length = x.shape
        x = x[None]
        bit = n // 2
        while bit:
            got = exchange(x, axis, bit, members)
            mine = (at // bit) % 2
            low = jnp.where(mine == 0, x, got)
            high = jnp.where(mine == 0, got, x)
            x = jnp.stack([low, high], axis=1).reshape(-1, w, length)
            bit //= 2
        return x.reshape(n * w, length)

    def product(a, dims):
        return lax.dot_general(
            a, block, (dims, ((), ())), precision=lax.Precision.HIGH, preferred_element_type=jnp.float32
        )

    driven = lax.optimization_barrier(excitation.transpose(0, 2, 1))
    driven = driven.reshape(STEPS, finest, CHUNKS, width, tests)
    waiting = pending[0].T.reshape(finest // rows, CHUNKS, width, tests)
    gain = sheet_gain[None, :]
    held, updated, arrived = [], [], {}

    def future_at(s):
        stage = s - SKEW * d
        source = s - CHUNKS + SKEW
        got = shift(updated[source], -1, [dd for dd in active(source) if dd > 0]) if source >= 0 else None
        arrived[s] = got
        if s >= CHUNKS + SKEW * (groups - 1):
            return got
        first = lax.dynamic_index_in_dim(waiting, jnp.clip(stage, 0, CHUNKS - 1), 1, keepdims=False)
        first = first.reshape(-1, tests)
        return first if got is None else jnp.where(stage < CHUNKS, first, got)

    for s in range(slots):
        members = active(s)
        tail = [dd for dd in members if dd > 0]
        future = future_at(s)
        current = shift(held[s - SKEW], 1, active(s - SKEW)) if s >= SKEW else None
        driving = whole = None
        if 0 in members:
            driving = gather(future, "row", [0])
        if tail:
            whole = gather(current, "col", tail)
        incident = driven[s // CHUNKS, :, s % CHUNKS].reshape(-1, tests) if driving is not None else None
        driving, whole, future, current, incident = lax.optimization_barrier(
            (driving, whole, future, current, incident)
        )
        fresh, new = current, future
        if driving is not None:
            driving = incident - driving
            part = lax.cond(
                is_head,
                lambda x: product(x, ((1,), (0,))),
                lambda x: jnp.zeros((x.shape[0], basis), jnp.float32),
                driving,
            )
        if whole is not None:
            field = lax.cond(
                is_head,
                lambda x: jnp.zeros((x.shape[0], tests), jnp.float32),
                lambda x: product(x, ((1,), (1,))),
                whole,
            )
        if driving is not None:
            sheet = scatter_sum(part, "col", [0])
            fresh = sheet / (1.0 + gain * sheet * sheet)
            if current is not None:
                fresh = jnp.where(is_head, fresh, current)
        if whole is not None:
            new = future + scatter_sum(field, "row", tail)
        fresh, new = lax.optimization_barrier((fresh, new))
        held.append(fresh)
        updated.append(new)

    for s in range(slots, stages + CHUNKS + SKEW * (groups - 2)):
        future_at(s)

    def outputs_of(dd):
        def build(held, got):
            mine = held[SKEW * dd : SKEW * dd + stages]
            now = jnp.stack(mine).reshape(STEPS, CHUNKS, finest // cols, width, basis)
            now = now.transpose(0, 4, 2, 1, 3).reshape(STEPS, basis, -1)
            if dd == groups - 1:
                return now, jnp.zeros((1, tests, pending.shape[2]), jnp.float32)
            last = [got[stages + SKEW * dd + i - stages] for i in range(CHUNKS)]
            last = jnp.stack(last).reshape(CHUNKS, finest // rows, width, tests)
            return now, last.transpose(3, 1, 0, 2).reshape(1, tests, -1)

        return build

    got = [arrived[s] for s in range(stages, stages + CHUNKS + SKEW * (groups - 2))]
    return lax.switch(d, [outputs_of(dd) for dd in range(groups)], held, got)


def solution(mesh):
    in_specs = (P("delay", "col", "row"), P(None, "col", None), P("delay", "col", "row"), P("row"))
    out_specs = (P(None, "row", "col"), P("delay", "col", "row"))
    return jax.shard_map(local, mesh=mesh, in_specs=in_specs, out_specs=out_specs, check_vma=False)
```

```python
import jax
import jax.numpy as jnp
from jax import lax
from jax.sharding import PartitionSpec as P

STEPS = 3
CHUNKS = 2
SKEW = 1
AXES = ("delay", "row", "col")


def local(operators, excitation, pending, sheet_gain):
    block = operators[0]
    groups, rows, cols = (lax.axis_size(a) for a in AXES)
    d, r, c = (lax.axis_index(a) for a in AXES)
    is_head = d == 0
    tests, basis = block.shape
    finest = max(rows, cols)
    width = excitation.shape[2] // (finest * CHUNKS)
    stages = STEPS * CHUNKS
    slots = stages + SKEW * (groups - 1)

    def place(dd, rr, cc):
        return (dd * rows + rr) * cols + cc

    def active(s):
        return [dd for dd in range(groups) if 0 <= s - SKEW * dd < stages]

    def exchange(x, axis, bit, members):
        pairs = []
        for dd in members:
            for rr in range(rows):
                for cc in range(cols):
                    to = (dd, rr ^ bit, cc) if axis == "row" else (dd, rr, cc ^ bit)
                    pairs.append((place(dd, rr, cc), place(*to)))
        return lax.ppermute(x, AXES, pairs)

    def shift(x, step, members):
        pairs = [
            (place(dd, rr, cc), place(dd + step, rr, cc))
            for dd in members
            if 0 <= dd + step < groups
            for rr in range(rows)
            for cc in range(cols)
        ]
        return lax.ppermute(x, AXES, pairs) if pairs else jnp.zeros_like(x)

    def scatter_sum(x, axis, members):
        n = lax.axis_size(axis)
        at = r if axis == "row" else c
        w = x.shape[0] // n
        x = x.reshape(n, w, -1)
        bit = 1
        while bit < n:
            x = x.reshape(x.shape[0] // 2, 2, w, -1)
            mine = (at // bit) % 2
            kept = lax.dynamic_index_in_dim(x, mine, 1, keepdims=False)
            other = lax.dynamic_index_in_dim(x, 1 - mine, 1, keepdims=False)
            x = kept + exchange(other, axis, bit, members)
            bit *= 2
        return x[0]

    def gather(x, axis, members):
        n = lax.axis_size(axis)
        at = r if axis == "row" else c
        w, length = x.shape
        x = x[None]
        bit = n // 2
        while bit:
            got = exchange(x, axis, bit, members)
            mine = (at // bit) % 2
            low = jnp.where(mine == 0, x, got)
            high = jnp.where(mine == 0, got, x)
            x = jnp.stack([low, high], axis=1).reshape(-1, w, length)
            bit //= 2
        return x.reshape(n * w, length)

    def product(a, dims):
        return lax.dot_general(
            a, block, (dims, ((), ())), precision=lax.Precision.HIGH, preferred_element_type=jnp.float32
        )

    def radiate(x):
        turned = lax.optimization_barrier(x.T)
        field = jnp.dot(block, turned, precision=lax.Precision.HIGH, preferred_element_type=jnp.float32)
        return lax.optimization_barrier(field).T

    driven = lax.optimization_barrier(excitation.transpose(0, 2, 1))
    driven = driven.reshape(STEPS, finest, CHUNKS, width, tests)
    waiting = pending[0].T.reshape(finest // rows, CHUNKS, width, tests)
    gain = sheet_gain[None, :]
    held, updated, arrived = [], [], {}

    def future_at(s):
        stage = s - SKEW * d
        source = s - CHUNKS + SKEW
        got = shift(updated[source], -1, [dd for dd in active(source) if dd > 0]) if source >= 0 else None
        arrived[s] = got
        if s >= CHUNKS + SKEW * (groups - 1):
            return got
        first = lax.dynamic_index_in_dim(waiting, jnp.clip(stage, 0, CHUNKS - 1), 1, keepdims=False)
        first = first.reshape(-1, tests)
        return first if got is None else jnp.where(stage < CHUNKS, first, got)

    for s in range(slots):
        members = active(s)
        tail = [dd for dd in members if dd > 0]
        future = future_at(s)
        current = shift(held[s - SKEW], 1, active(s - SKEW)) if s >= SKEW else None
        driving = whole = None
        if 0 in members:
            driving = gather(future, "row", [0])
        if tail:
            whole = gather(current, "col", tail)
        incident = driven[s // CHUNKS, :, s % CHUNKS].reshape(-1, tests) if driving is not None else None
        driving, whole, future, current, incident = lax.optimization_barrier(
            (driving, whole, future, current, incident)
        )
        fresh, new = current, future
        if driving is not None:
            driving = incident - driving
            part = lax.cond(
                is_head,
                lambda x: product(x, ((1,), (0,))),
                lambda x: jnp.zeros((x.shape[0], basis), jnp.float32),
                driving,
            )
        if whole is not None:
            field = lax.cond(
                is_head,
                lambda x: jnp.zeros((x.shape[0], tests), jnp.float32),
                radiate,
                whole,
            )
        if driving is not None:
            sheet = scatter_sum(part, "col", [0])
            fresh = sheet / (1.0 + gain * sheet * sheet)
            if current is not None:
                fresh = jnp.where(is_head, fresh, current)
        if whole is not None:
            new = future + scatter_sum(field, "row", tail)
        fresh, new = lax.optimization_barrier((fresh, new))
        held.append(fresh)
        updated.append(new)

    for s in range(slots, stages + CHUNKS + SKEW * (groups - 2)):
        future_at(s)

    def outputs_of(dd):
        def build(held, got):
            mine = held[SKEW * dd : SKEW * dd + stages]
            now = jnp.stack(mine).reshape(STEPS, CHUNKS, finest // cols, width, basis)
            now = now.transpose(0, 4, 2, 1, 3).reshape(STEPS, basis, -1)
            if dd == groups - 1:
                return now, jnp.zeros((1, tests, pending.shape[2]), jnp.float32)
            last = [got[stages + SKEW * dd + i - stages] for i in range(CHUNKS)]
            last = jnp.stack(last).reshape(CHUNKS, finest // rows, width, tests)
            return now, last.transpose(3, 1, 0, 2).reshape(1, tests, -1)

        return build

    got = [arrived[s] for s in range(stages, stages + CHUNKS + SKEW * (groups - 2))]
    return lax.switch(d, [outputs_of(dd) for dd in range(groups)], held, got)


def solution(mesh):
    in_specs = (P("delay", "col", "row"), P(None, "col", None), P("delay", "col", "row"), P("row"))
    out_specs = (P(None, "row", "col"), P("delay", "col", "row"))
    return jax.shard_map(local, mesh=mesh, in_specs=in_specs, out_specs=out_specs, check_vma=False)
```
